32 devices in a mesh: fsdp: 8 (over z, core), tp: 4 (over y, x).
Axes of the slice: x: 2, y: 2, z: 4, core: 2. Of those that a mesh axis runs over, the one named last changes fastest.
Arguments:
- inputs: float32 [8192, 1024], P(('fsdp', 'tp')), may hold values from -40 to 40
- segment_ids: int32 [8, 1024], P('fsdp'), may hold values from 0 to 15, never falling along the last dimension, each value on 1 to 512 neighbouring positions
- attn_norm: bfloat16 [2, 1024], P(None, 'fsdp'), may hold values from 0.25 to 1.75
- mlp_norm: bfloat16 [2, 1024], P(None, 'fsdp'), may hold values from 0.25 to 1.75
- query_norm: bfloat16 [2, 128], P(None, 'fsdp'), may hold values from 0.25 to 1.75
- key_norm: bfloat16 [2, 128], P(None, 'fsdp'), may hold values from 0.25 to 1.75
- w_query: bfloat16 [2, 1024, 2048], P(None, 'fsdp', 'tp'), may hold values from -0.1875 to 0.1875
- w_key: bfloat16 [2, 1024, 1024], P(None, 'fsdp', 'tp'), may hold values from -0.1875 to 0.1875
- w_value: bfloat16 [2, 1024, 1024], P(None, 'fsdp', 'tp'), may hold values from -0.1875 to 0.1875
- w_out: bfloat16 [2, 2048, 1024], P(None, 'tp', 'fsdp'), may hold values from -0.5 to 0.5
- w_gate: bfloat16 [2, 1024, 3072], P(None, 'fsdp', 'tp'), may hold values from -0.1875 to 0.1875
- w_up: bfloat16 [2, 1024, 3072], P(None, 'fsdp', 'tp'), may hold values from -0.1875 to 0.1875
- w_down: bfloat16 [2, 3072, 1024], P(None, 'tp', 'fsdp'), may hold values from -0.15625 to 0.15625
- cotangent: float32 [8192, 1024], P(('fsdp', 'tp')), may hold values from -6 to 6
Outputs:
- outputs: float32 [8192, 1024], P(('fsdp', 'tp'))
- input_grad: float32 [8192, 1024], P(('fsdp', 'tp'))
- grad_query: float32 [2, 1024, 2048], P(None, 'fsdp', 'tp')
- grad_key: float32 [2, 1024, 1024], P(None, 'fsdp', 'tp')
- grad_value: float32 [2, 1024, 1024], P(None, 'fsdp', 'tp')
- grad_out: float32 [2, 2048, 1024], P(None, 'tp', 'fsdp')
- grad_gate: float32 [2, 1024, 3072], P(None, 'fsdp', 'tp')
- grad_up: float32 [2, 1024, 3072], P(None, 'fsdp', 'tp')
- grad_down: float32 [2, 3072, 1024], P(None, 'tp', 'fsdp')
- grad_attn_norm: float32 [2, 1024], P(None, 'fsdp')
- grad_mlp_norm: float32 [2, 1024], P(None, 'fsdp')
- grad_query_norm: float32 [2, 128], P(None, 'fsdp')
- grad_key_norm: float32 [2, 128], P(None, 'fsdp')
The draws below stay inside these ranges and needn't reach their ends.
Inputs may be any that keep to these rules, and one draw needn't show every extreme that they name: `segment_ids`: document numbers within each row start at 0 and never fall.
All inputs are finite; a program needn't handle non-finite values.
Results may differ from the reference program's by a relative error of at most 0.03.
Values may be sent and summed in bfloat16 or wider, within the bound.
A program may use at most 256 MiB of HBM per device.

```python
import math
import jax
import jax.numpy as jnp
import numpy as np
from jax import lax

D = 1024
H = 16
KV = 8
HD = 128
FF = 3072
LAYERS = 2
LEN = 1024
SEQS = 8
TOKENS = 8192


def draw_inputs(key, part):
    base_key = jax.random.fold_in(key, 11)
    noise_key, row_key, column_key = jax.random.split(base_key, 3)
    row_scale = jnp.exp(jax.random.uniform(row_key, (TOKENS, 1), jnp.float32) * math.log(10.0))
    column_scale = jnp.exp(jax.random.uniform(column_key, (1, D), jnp.float32) * math.log(10.0))
    noise = jax.random.normal(noise_key, (TOKENS, D), jnp.float32)
    noise = jnp.clip(noise, -4.0, 4.0)
    return noise * row_scale * column_scale * 0.1


def levels(key, extent, shards, smallest, high):
    gain = 1.0
    for position, parts in shards:
        steps = jax.random.uniform(jax.random.fold_in(jax.random.fold_in(key, 6), position), (parts,), jnp.float32, smallest / len(shards), high / len(shards))
        gain = gain * jnp.repeat(jnp.exp(steps), extent[position] // parts).reshape((-1,) + (1,) * (len(extent) - 1 - position))
    return gain


def profile(amount, total, limit, skew):
    weights = [(1 << 20) // math.isqrt(grade ** skew) + 1 for grade in range(2, amount + 1)]
    surplus, counts = total - limit - (amount - 1), [1] * (amount - 1)
    while surplus > 0:
        movable = [i for i in range(amount - 1) if counts[i] < limit]
        mass, left = sum([weights[i] for i in movable]), surplus
        for i in movable:
            addition = min(limit - counts[i], max(1, left * weights[i] // mass), surplus)
            counts[i] = counts[i] + addition
            surplus = surplus - addition
    return np.array([limit] + counts)


def uneven_parts(stream_key, number_of, total, most, slope):
    if number_of == 2:
        one = jax.random.randint(stream_key, (), max(1, total - most), min(most, total - 1) + 1)
        return jnp.stack([one, total - one])
    lengths = jnp.asarray(profile(number_of, total, most, slope), jnp.int32)
    pairs = (number_of - 1) // 2
    source_of, receiver = lengths[1:1 + 2 * pairs:2], lengths[2:2 + 2 * pairs:2]
    room = jnp.minimum(source_of - 1, most - receiver)
    shifted = jax.random.randint(jax.random.fold_in(stream_key, 1), (pairs,), 0, 1 << 20) % (room + 1)
    lengths = lengths.at[1:1 + 2 * pairs:2].set(source_of - shifted).at[2:2 + 2 * pairs:2].set(receiver + shifted)
    return lengths[jax.random.permutation(jax.random.fold_in(stream_key, 2), number_of)]


def normal_values(key, dims, width, bound, cuts=(), kind=jnp.bfloat16):
    gain = levels(key, dims, cuts, -0.22, 0.18) if cuts else 1.0
    entries = jax.random.normal(key, dims, jnp.float32) * width * gain
    return jnp.minimum(jnp.maximum(entries, -bound), bound).astype(kind)


def setup_inputs(seed: int = 0) -> dict:
    seeds = jax.random.split(jax.random.key(seed), 15)
    return {
        "inputs": draw_inputs(jax.random.fold_in(seeds[14], 71), 0),
        "segment_ids": jax.vmap(lambda own: jnp.searchsorted(jnp.cumsum(uneven_parts(own, max(4, LEN // 64), LEN, LEN // 2, 1)), jnp.arange(LEN), side="right"))(jax.random.split(seeds[1], SEQS)).reshape((SEQS, LEN)).astype(jnp.int32),
        "attn_norm": jnp.clip(1.0 + 0.15 * jax.random.normal(seeds[2], (LAYERS, D), jnp.float32), 0.25, 1.75).astype(jnp.bfloat16),
        "mlp_norm": jnp.clip(1.0 + 0.15 * jax.random.normal(seeds[3], (LAYERS, D), jnp.float32), 0.25, 1.75).astype(jnp.bfloat16),
        "query_norm": jnp.clip(1.0 + 0.15 * jax.random.normal(seeds[4], (LAYERS, HD), jnp.float32), 0.25, 1.75).astype(jnp.bfloat16),
        "key_norm": jnp.clip(1.0 + 0.15 * jax.random.normal(seeds[5], (LAYERS, HD), jnp.float32), 0.25, 1.75).astype(jnp.bfloat16),
        "w_query": normal_values(seeds[6], (LAYERS, D, H * HD), D ** -0.5, 0.1875, ((1, 8), (2, 4))),
        "w_key": normal_values(seeds[7], (LAYERS, D, KV * HD), D ** -0.5, 0.1875, ((1, 8), (2, 4))),
        "w_value": normal_values(seeds[8], (LAYERS, D, KV * HD), D ** -0.5, 0.1875, ((1, 8), (2, 4))),
        "w_out": normal_values(seeds[9], (LAYERS, H * HD, D), (H * HD // 16) ** -0.5, 0.5, ((1, 4), (2, 8))),
        "w_gate": normal_values(seeds[10], (LAYERS, D, FF), D ** -0.5, 0.1875, ((1, 8), (2, 4))),
        "w_up": normal_values(seeds[11], (LAYERS, D, FF), D ** -0.5, 0.1875, ((1, 8), (2, 4))),
        "w_down": normal_values(seeds[12], (LAYERS, FF, D), (FF // 2) ** -0.5, 0.15625, ((1, 4), (2, 8))),
        "cotangent": normal_values(seeds[13], (TOKENS, D), 1.0, 6.0, ((0, 32),), jnp.float32),
    }


epsilon = 1e-06
theta_base = 1000000.0

def rounded(operand):
    return lax.optimization_barrier(operand.astype(jnp.bfloat16)).astype(jnp.float32)

def mat_dot(left_arg, right_arg):
    return jnp.dot(left_arg, right_arg, preferred_element_type=jnp.float32)

def dot_left_t(left_arg, right_arg):
    return lax.dot_general(left_arg, right_arg, (((0,), (0,)), ((), ())), preferred_element_type=jnp.float32)

def dot_right_t(left_arg, right_arg):
    return lax.dot_general(left_arg, right_arg, (((1,), (1,)), ((), ())), preferred_element_type=jnp.float32)

def positions_of(segment_ids):
    token_index = jnp.broadcast_to(jnp.arange(segment_ids.shape[1], dtype=jnp.int32)[None, :], segment_ids.shape)
    first_flag = jnp.concatenate([jnp.ones((segment_ids.shape[0], 1), dtype=jnp.bool_), segment_ids[:, 1:] != segment_ids[:, :-1]], axis=1)
    starts = lax.cummax(jnp.where(first_flag, token_index, jnp.zeros_like(token_index)), axis=1)
    return (token_index - starts).reshape(-1)

def rope_tables(positions, head_dim):
    half_dim = head_dim // 2
    frequency = jnp.exp(jnp.arange(half_dim, dtype=jnp.float32) * (-2.0 * math.log(theta_base) / head_dim))
    angles = positions.astype(jnp.float32)[:, None] * frequency[None, :]
    return (jnp.cos(angles)[:, None, :], jnp.sin(angles)[:, None, :])

def rope_apply(operand, cosine, sine_part):
    half_dim = operand.shape[-1] // 2
    first_half = operand[..., :half_dim]
    second_half = operand[..., half_dim:]
    return jnp.concatenate([first_half * cosine - second_half * sine_part, second_half * cosine + first_half * sine_part], axis=-1)

def rope_back(operand, cosine, sine_part):
    half_dim = operand.shape[-1] // 2
    first_half = operand[..., :half_dim]
    second_half = operand[..., half_dim:]
    return jnp.concatenate([first_half * cosine + second_half * sine_part, second_half * cosine - first_half * sine_part], axis=-1)

def row_norm(operand, gain_vec):
    scale_part = lax.rsqrt(lax.optimization_barrier(jnp.mean(operand * operand, axis=-1, keepdims=True)) + epsilon)
    hat_part = operand * scale_part
    return (hat_part * gain_vec.astype(jnp.float32), hat_part, scale_part)

def norm_back(grad_normed, hat_part, scale_part, gain_vec, sum_axes):
    scaled = grad_normed * gain_vec.astype(jnp.float32)
    grad_in = scale_part * (scaled - hat_part * lax.optimization_barrier(jnp.mean(scaled * hat_part, axis=-1, keepdims=True)))
    grad_gain = lax.optimization_barrier(jnp.sum(grad_normed * hat_part, axis=sum_axes))
    return (grad_in, grad_gain)

def visible_mask(segment_row):
    token_index = jnp.arange(segment_row.shape[0], dtype=jnp.int32)
    return (segment_row[:, None] == segment_row[None, :]) & (token_index[None, :] <= token_index[:, None])

def score_probs(q_rot, k_rot, segment_row):
    score_scale = q_rot.shape[-1] ** (-0.5)
    scores = jnp.einsum('qkgd,tkd->kgqt', q_rot.astype(jnp.float32), k_rot.astype(jnp.float32)) * score_scale
    return (scores, visible_mask(segment_row), score_scale)

def attend_bundle(bundle):
    q_rot, k_rot, values, segment_row = bundle
    scores, allowed, score_scale = score_probs(q_rot, k_rot, segment_row)
    totals = lax.optimization_barrier(jnp.sum(jnp.where(allowed, jnp.exp(scores), 0.0), axis=-1))
    log_total = jnp.log(totals)
    attn_probs = jnp.where(allowed, jnp.exp(scores - log_total[..., None]), 0.0)
    attended = jnp.einsum('kgqt,tkd->qkgd', rounded(attn_probs), values.astype(jnp.float32)).astype(jnp.bfloat16)
    return (attended, log_total)

def back_bundle(bundle):
    q_rot, k_rot, values, segment_row, log_total, grad_attended = bundle
    scores, allowed, score_scale = score_probs(q_rot, k_rot, segment_row)
    attn_probs = jnp.where(allowed, jnp.exp(scores - log_total[..., None]), 0.0)
    grad_wide = grad_attended.astype(jnp.float32)
    grad_values = jnp.einsum('kgqt,qkgd->tkd', rounded(attn_probs), grad_wide).astype(jnp.bfloat16)
    grad_probs = jnp.einsum('qkgd,tkd->kgqt', grad_wide, values.astype(jnp.float32))
    row_delta = lax.optimization_barrier(jnp.sum(attn_probs * grad_probs, axis=-1, keepdims=True))
    grad_scores = rounded(attn_probs * (grad_probs - row_delta) * score_scale)
    grad_q_rot = jnp.einsum('kgqt,tkd->qkgd', grad_scores, k_rot.astype(jnp.float32))
    grad_k_rot = jnp.einsum('kgqt,qkgd->tkd', grad_scores, q_rot.astype(jnp.float32))
    return (grad_q_rot, grad_k_rot, grad_values)

def layer_forward(resid, segment_ids, cosine, sine_part, weights):
    w_query, w_key, w_value, w_out, w_gate, w_up, w_down, attn_gain, mlp_gain, query_gain, key_gain = weights
    seq_count, length = segment_ids.shape
    head_dim = query_gain.shape[0]
    q_heads = w_query.shape[1] // head_dim
    kv_heads = w_key.shape[1] // head_dim
    group_size = q_heads // kv_heads
    normed, hat_attn, scale_attn = row_norm(resid, attn_gain)
    attn_rows = normed.astype(jnp.bfloat16)
    token_count = attn_rows.shape[0]
    queries = mat_dot(attn_rows, w_query).reshape(token_count, q_heads, head_dim)
    keys_raw = mat_dot(attn_rows, w_key).reshape(token_count, kv_heads, head_dim)
    values = mat_dot(attn_rows, w_value).astype(jnp.bfloat16)
    query_normed, query_hat, query_scale = row_norm(queries, query_gain)
    key_normed, key_hat, key_scale = row_norm(keys_raw, key_gain)
    q_rot = rope_apply(query_normed, cosine, sine_part).astype(jnp.bfloat16)
    k_rot = rope_apply(key_normed, cosine, sine_part).astype(jnp.bfloat16)
    attended, log_total = lax.map(attend_bundle, (q_rot.reshape(seq_count, length, kv_heads, group_size, head_dim), k_rot.reshape(seq_count, length, kv_heads, head_dim), values.reshape(seq_count, length, kv_heads, head_dim), segment_ids))
    attended = attended.reshape(token_count, q_heads * head_dim)
    resid_mid = resid + mat_dot(attended, w_out)
    normed_mlp, hat_mlp, scale_mlp = row_norm(resid_mid, mlp_gain)
    mlp_rows = normed_mlp.astype(jnp.bfloat16)
    gate_act = mat_dot(mlp_rows, w_gate)
    up_act = mat_dot(mlp_rows, w_up)
    hidden_act = (jax.nn.silu(gate_act) * up_act).astype(jnp.bfloat16)
    resid_next = resid_mid + mat_dot(hidden_act, w_down)
    kept_state = (hat_attn, scale_attn, attn_rows, query_hat, query_scale, key_hat, key_scale, q_rot, k_rot, values, log_total, attended, hat_mlp, scale_mlp, mlp_rows, gate_act, up_act, hidden_act)
    return (resid_next, kept_state)

def layer_backward(grad_resid, segment_ids, cosine, sine_part, weights, kept_state):
    w_query, w_key, w_value, w_out, w_gate, w_up, w_down, attn_gain, mlp_gain, query_gain, key_gain = weights
    hat_attn, scale_attn, attn_rows, query_hat, query_scale, key_hat, key_scale, q_rot, k_rot, values, log_total, attended, hat_mlp, scale_mlp, mlp_rows, gate_act, up_act, hidden_act = kept_state
    seq_count, length = segment_ids.shape
    head_dim = query_gain.shape[0]
    q_heads = w_query.shape[1] // head_dim
    kv_heads = w_key.shape[1] // head_dim
    group_size = q_heads // kv_heads
    token_count = attn_rows.shape[0]
    grad_half = grad_resid.astype(jnp.bfloat16)
    grad_down = dot_left_t(hidden_act, grad_half)
    grad_hidden = dot_right_t(grad_half, w_down)
    sigmoid_gate = jax.nn.sigmoid(gate_act)
    grad_gate_act = (grad_hidden * up_act * sigmoid_gate * (1.0 + gate_act * (1.0 - sigmoid_gate))).astype(jnp.bfloat16)
    grad_up_act = (grad_hidden * gate_act * sigmoid_gate).astype(jnp.bfloat16)
    grad_gate = dot_left_t(mlp_rows, grad_gate_act)
    grad_up = dot_left_t(mlp_rows, grad_up_act)
    grad_normed_mlp = dot_right_t(grad_gate_act, w_gate) + dot_right_t(grad_up_act, w_up)
    grad_norm_in, grad_mlp_gain = norm_back(grad_normed_mlp, hat_mlp, scale_mlp, mlp_gain, (0,))
    grad_mid = grad_resid + grad_norm_in
    grad_mid_half = grad_mid.astype(jnp.bfloat16)
    grad_out = dot_left_t(attended, grad_mid_half)
    grad_attended = dot_right_t(grad_mid_half, w_out).astype(jnp.bfloat16)
    grad_q_rot, grad_k_rot, grad_values = lax.map(back_bundle, (q_rot.reshape(seq_count, length, kv_heads, group_size, head_dim), k_rot.reshape(seq_count, length, kv_heads, head_dim), values.reshape(seq_count, length, kv_heads, head_dim), segment_ids, log_total, grad_attended.reshape(seq_count, length, kv_heads, group_size, head_dim)))
    grad_qn = rope_back(grad_q_rot.reshape(token_count, q_heads, head_dim), cosine, sine_part)
    grad_kn = rope_back(grad_k_rot.reshape(token_count, kv_heads, head_dim), cosine, sine_part)
    grad_queries_wide, grad_query_gain = norm_back(grad_qn, query_hat, query_scale, query_gain, (0, 1))
    grad_keys_wide, grad_key_gain = norm_back(grad_kn, key_hat, key_scale, key_gain, (0, 1))
    grad_queries = grad_queries_wide.reshape(token_count, q_heads * head_dim).astype(jnp.bfloat16)
    grad_keys = grad_keys_wide.reshape(token_count, kv_heads * head_dim).astype(jnp.bfloat16)
    grad_values = grad_values.reshape(token_count, kv_heads * head_dim)
    grad_query = dot_left_t(attn_rows, grad_queries)
    grad_key = dot_left_t(attn_rows, grad_keys)
    grad_value = dot_left_t(attn_rows, grad_values)
    grad_normed_attn = dot_right_t(grad_queries, w_query) + dot_right_t(grad_keys, w_key) + dot_right_t(grad_values, w_value)
    grad_attn_in, grad_attn_gain = norm_back(grad_normed_attn, hat_attn, scale_attn, attn_gain, (0,))
    grad_in = grad_mid + grad_attn_in
    return (grad_in, (grad_query, grad_key, grad_value, grad_out, grad_gate, grad_up, grad_down, grad_attn_gain, grad_mlp_gain, grad_query_gain, grad_key_gain))

def reference(inputs, segment_ids, attn_norm, mlp_norm, query_norm, key_norm, w_query, w_key, w_value, w_out, w_gate, w_up, w_down, cotangent):
    positions = positions_of(segment_ids)
    cosine, sine_part = rope_tables(positions, query_norm.shape[1])
    layer_count = w_query.shape[0]
    resid = inputs
    layers_kept = []
    for layer_idx in range(layer_count):
        full_weights = (w_query[layer_idx], w_key[layer_idx], w_value[layer_idx], w_out[layer_idx], w_gate[layer_idx], w_up[layer_idx], w_down[layer_idx], attn_norm[layer_idx], mlp_norm[layer_idx], query_norm[layer_idx], key_norm[layer_idx])
        resid, kept_state = layer_forward(resid, segment_ids, cosine, sine_part, full_weights)
        layers_kept.append((full_weights, kept_state))
    outputs = resid
    grad_resid = cotangent
    grads_list = []
    for layer_idx in reversed(range(layer_count)):
        full_weights, kept_state = layers_kept[layer_idx]
        grad_resid, grad_parts = layer_backward(grad_resid, segment_ids, cosine, sine_part, full_weights, kept_state)
        grads_list.insert(0, grad_parts)
    stacked = [jnp.stack([grads_list[layer_idx][slot_index] for layer_idx in range(layer_count)]) for slot_index in range(11)]
    return (outputs, grad_resid, stacked[0], stacked[1], stacked[2], stacked[3], stacked[4], stacked[5], stacked[6], stacked[7], stacked[8], stacked[9], stacked[10])
```

```python
import functools
import math

import jax
import jax.numpy as jnp
from jax import lax
from jax.experimental import pallas as pl
from jax.experimental.pallas import tpu as pltpu
from jax.sharding import PartitionSpec as P

HD = 128
DOC_MAX = 512


epsilon = 1e-06
theta_base = 1000000.0


def mat_dot(left_arg, right_arg):
    return jnp.dot(left_arg, right_arg, preferred_element_type=jnp.float32)


def dot_left_t(left_arg, right_arg):
    return lax.dot_general(
        left_arg, right_arg, (((0,), (0,)), ((), ())), preferred_element_type=jnp.float32
    )


def dot_right_t(left_arg, right_arg):
    return lax.dot_general(
        left_arg, right_arg, (((1,), (1,)), ((), ())), preferred_element_type=jnp.float32
    )


def positions_of(segment_ids):
    token_index = jnp.arange(segment_ids.shape[1], dtype=jnp.int32)[None, :]
    first_flag = jnp.concatenate(
        [
            jnp.ones((segment_ids.shape[0], 1), dtype=jnp.bool_),
            segment_ids[:, 1:] != segment_ids[:, :-1],
        ],
        axis=1,
    )
    starts = lax.cummax(jnp.where(first_flag, token_index, jnp.zeros_like(token_index)), axis=1)
    return (token_index - starts).reshape(-1)


def rope_tables(positions, head_dim):
    half_dim = head_dim // 2
    frequency = jnp.exp(
        jnp.arange(half_dim, dtype=jnp.float32) * (-2.0 * math.log(theta_base) / head_dim)
    )
    angles = positions.astype(jnp.float32)[:, None] * frequency[None, :]
    return (jnp.cos(angles)[:, None, :], jnp.sin(angles)[:, None, :])


def row_norm(operand, gain_vec):
    scale_part = lax.rsqrt(jnp.mean(operand * operand, axis=-1, keepdims=True) + epsilon)
    hat_part = operand * scale_part
    return (hat_part * gain_vec, hat_part, scale_part)


def norm_back(grad_normed, hat_part, scale_part, gain_vec, sum_axes):
    scaled = grad_normed * gain_vec
    grad_in = scale_part * (scaled - hat_part * jnp.mean(scaled * hat_part, axis=-1, keepdims=True))
    grad_gain = jnp.sum(grad_normed * hat_part, axis=sum_axes)
    return (grad_in, grad_gain)


def head_rot(operand, gain_row, cos_wide, sin_wide):
    normed, hat_part, scale_part = row_norm(operand, gain_row)
    rotated = normed * cos_wide + pltpu.roll(normed, HD // 2, 1) * sin_wide
    return rotated.astype(jnp.bfloat16), hat_part, scale_part


def head_back(grad_rot, hat_part, scale_part, gain_row, cos_wide, sin_wide):
    grad_n = grad_rot * cos_wide - pltpu.roll(grad_rot, HD // 2, 1) * sin_wide
    grad_in, grad_gain = norm_back(grad_n, hat_part, scale_part, gain_row, (0,))
    return grad_in.astype(jnp.bfloat16), grad_gain[None, :]


def block_exp(q_blk, k_win, seg_col, seg_row, row_lo, key_lo):
    rows, keys = q_blk.shape[0], k_win.shape[0]
    scores = dot_right_t(q_blk, k_win) * (HD ** (-0.5))
    u_idx = row_lo + lax.broadcasted_iota(jnp.int32, (rows, keys), 0)
    t_idx = key_lo + lax.broadcasted_iota(jnp.int32, (rows, keys), 1)
    allowed = (seg_col == seg_row) & (t_idx <= u_idx)
    powers = jnp.where(allowed, jnp.exp(scores), 0.0)
    return powers / jnp.sum(powers, axis=-1, keepdims=True)


def attend_kernel(group, rows, q_ref, k_ref, v_ref, cos_ref, sin_ref, gain_ref, sc_ref, sr_ref, o_ref):
    length = k_ref.shape[0]
    gain_q, gain_k = gain_ref[0:1, :], gain_ref[1:2, :]
    k_rot, _, _ = head_rot(k_ref[...], gain_k, cos_ref[...], sin_ref[...])
    values = v_ref[...].astype(jnp.bfloat16)
    for lo in range(0, length, rows):
        hi = lo + rows
        key_lo = max(0, lo - DOC_MAX)
        for g in range(group):
            lanes = slice(g * HD, (g + 1) * HD)
            q_rot, _, _ = head_rot(
                q_ref[lo:hi, lanes], gain_q, cos_ref[lo:hi, :], sin_ref[lo:hi, :]
            )
            probs = block_exp(
                q_rot, k_rot[key_lo:hi], sc_ref[lo:hi, :], sr_ref[0, :, key_lo:hi], lo, key_lo
            )
            o_ref[lo:hi, lanes] = mat_dot(probs.astype(jnp.bfloat16), values[key_lo:hi]).astype(
                jnp.bfloat16
            )


def attend_back_kernel(
    group, rows, heads, kv, q_ref, k_ref, v_ref, cos_ref, sin_ref, gain_ref, sc_ref, sr_ref,
    da_ref, out_ref, gg_ref, dk_ref, dv_ref,
):
    length = k_ref.shape[0]
    kv_idx = pl.program_id(1)
    gain_q, gain_k = gain_ref[0:1, :], gain_ref[1:2, :]
    k_rot, k_hat, k_scale = head_rot(k_ref[...], gain_k, cos_ref[...], sin_ref[...])
    values = v_ref[...].astype(jnp.bfloat16)
    dk_ref[...] = jnp.zeros_like(dk_ref)
    dv_ref[...] = jnp.zeros_like(dv_ref)
    gq_total = jnp.zeros((1, HD), jnp.float32)
    scale = HD ** (-0.5)
    for lo in range(0, length, rows):
        hi = lo + rows
        key_lo = max(0, lo - DOC_MAX)
        k_win, v_win = k_rot[key_lo:hi], values[key_lo:hi]
        for g in range(group):
            lanes = slice(g * HD, (g + 1) * HD)
            cos_b, sin_b = cos_ref[lo:hi, :], sin_ref[lo:hi, :]
            q_rot, q_hat, q_scale = head_rot(q_ref[lo:hi, lanes], gain_q, cos_b, sin_b)
            probs = block_exp(
                q_rot, k_win, sc_ref[lo:hi, :], sr_ref[0, :, key_lo:hi], lo, key_lo
            )
            da = da_ref[lo:hi, lanes]
            dv_ref[key_lo:hi, :] += dot_left_t(probs.astype(jnp.bfloat16), da)
            grad_probs = dot_right_t(da, v_win)
            delta = jnp.sum(probs * grad_probs, axis=-1, keepdims=True)
            ds = (probs * (grad_probs - delta) * scale).astype(jnp.bfloat16)
            dk_ref[key_lo:hi, :] += dot_left_t(ds, q_rot)
            dq, gq = head_back(mat_dot(ds, k_win), q_hat, q_scale, gain_q, cos_b, sin_b)
            gq_total = gq_total + gq
            off = pl.multiple_of((kv_idx * group + g) * HD, HD)
            out_ref[lo:hi, pl.ds(off, HD)] = dq
    dk, gk = head_back(dk_ref[...], k_hat, k_scale, gain_k, cos_ref[...], sin_ref[...])
    out_ref[:, pl.ds(pl.multiple_of((heads + kv_idx) * HD, HD), HD)] = dk
    out_ref[:, pl.ds(pl.multiple_of((heads + kv + kv_idx) * HD, HD), HD)] = dv_ref[...].astype(
        jnp.bfloat16
    )

    @pl.when((pl.program_id(0) == 0) & (kv_idx == 0))
    def _():
        gg_ref[...] = jnp.zeros_like(gg_ref)

    gg_ref[0:1, :] += gq_total
    gg_ref[1:2, :] += gk


def head_specs(length, group, heads, kv):
    return [
        pl.BlockSpec((length, group * HD), lambda s, k: (s, k)),
        pl.BlockSpec((length, HD), lambda s, k: (s, heads + k)),
        pl.BlockSpec((length, HD), lambda s, k: (s, heads + kv + k)),
        pl.BlockSpec((length, HD), lambda s, k: (s, 0)),
        pl.BlockSpec((length, HD), lambda s, k: (s, 0)),
        pl.BlockSpec((8, HD), lambda s, k: (0, 0)),
        pl.BlockSpec((length, 1), lambda s, k: (s, 0)),
        pl.BlockSpec((1, 1, length), lambda s, k: (s, 0, 0)),
    ]


def attend(qkv, tables, gains, dims):
    heads, kv = dims
    cos_wide, sin_wide, seg_col, seg_row = tables
    seqs, _, length = seg_row.shape
    group = heads // kv
    rows = min(256, length)
    tokens = seqs * length
    return pl.pallas_call(
        functools.partial(attend_kernel, group, rows),
        grid=(seqs, kv),
        in_specs=head_specs(length, group, heads, kv),
        out_specs=pl.BlockSpec((length, group * HD), lambda s, k: (s, k)),
        out_shape=jax.ShapeDtypeStruct((tokens, heads * HD), jnp.bfloat16),
        cost_estimate=pl.CostEstimate(
            flops=4 * tokens * heads * HD * 640, bytes_accessed=qkv.size * 6, transcendentals=0
        ),
        compiler_params=pltpu.CompilerParams(vmem_limit_bytes=40 * 2**20),
        name="attend",
    )(qkv, qkv, qkv, cos_wide, sin_wide, gains, seg_col, seg_row)


def attend_back(qkv, tables, gains, dims, grad_attended):
    heads, kv = dims
    cos_wide, sin_wide, seg_col, seg_row = tables
    seqs, _, length = seg_row.shape
    group = heads // kv
    rows = min(256, length)
    tokens = seqs * length
    width = (heads + 2 * kv) * HD
    return pl.pallas_call(
        functools.partial(attend_back_kernel, group, rows, heads, kv),
        grid=(seqs, kv),
        in_specs=head_specs(length, group, heads, kv)
        + [pl.BlockSpec((length, group * HD), lambda s, k: (s, k))],
        out_specs=[
            pl.BlockSpec((length, width), lambda s, k: (s, 0)),
            pl.BlockSpec((8, HD), lambda s, k: (0, 0)),
        ],
        out_shape=[
            jax.ShapeDtypeStruct((tokens, width), jnp.bfloat16),
            jax.ShapeDtypeStruct((8, HD), jnp.float32),
        ],
        scratch_shapes=[pltpu.VMEM((length, HD), jnp.float32)] * 2,
        cost_estimate=pl.CostEstimate(
            flops=10 * tokens * heads * HD * 640, bytes_accessed=qkv.size * 8, transcendentals=0
        ),
        compiler_params=pltpu.CompilerParams(vmem_limit_bytes=48 * 2**20),
        name="attend_back",
    )(qkv, qkv, qkv, cos_wide, sin_wide, gains, seg_col, seg_row, grad_attended)


def spread_rows(local_rows):
    return lax.all_gather(local_rows, "tp", axis=0, tiled=True)


def sum_rows(partial_rows):
    return lax.psum_scatter(
        partial_rows.astype(jnp.bfloat16), "tp", scatter_dimension=0, tiled=True
    ).astype(jnp.float32)


def gather_weights(block):
    return lax.all_gather(block, "fsdp", axis=0, tiled=True)


def scatter_grads(block):
    return lax.psum_scatter(
        block.astype(jnp.bfloat16), "fsdp", scatter_dimension=0, tiled=True
    ).astype(jnp.float32)


def local(
    inputs, segment_ids, attn_norm, mlp_norm, query_norm, key_norm, w_query, w_key, w_value,
    w_out, w_gate, w_up, w_down, cotangent,
):
    layers = w_query.shape[0]
    fsdp = lax.axis_size("fsdp")
    fsdp_idx = lax.axis_index("fsdp")
    part = attn_norm.shape[1]
    small = query_norm.shape[1]
    q_w, kv_w = w_query.shape[2], w_key.shape[2]
    ff_w = w_gate.shape[2]
    dims = (q_w // HD, kv_w // HD)
    qkv_w = q_w + 2 * kv_w

    columns = []
    for l in range(layers):
        columns += [
            attn_norm[l],
            mlp_norm[l],
            jnp.pad(query_norm[l], (0, part - small)),
            jnp.pad(key_norm[l], (0, part - small)),
        ]
    gain_block = jnp.stack(columns, axis=1)
    gain_block = jnp.pad(gain_block, ((0, 0), (0, -gain_block.shape[1] % HD)))
    gain_w = gain_block.shape[1]

    def qkv_block(l):
        return [w_query[l], w_key[l], w_value[l]]

    def rest_block(l):
        return [w_out[l].T, w_gate[l], w_up[l], w_down[l].T]

    full = []
    for l in range(layers):
        lead = gather_weights(
            jnp.concatenate(qkv_block(l) + ([gain_block] if l == 0 else []), axis=1)
        )
        if l == 0:
            gain_all = lead[:, qkv_w:].T.astype(jnp.float32)
        rest = gather_weights(jnp.concatenate(rest_block(l), axis=1))
        full.append(
            (
                lead[:, :qkv_w],
                rest[:, :q_w],
                rest[:, q_w : q_w + ff_w],
                rest[:, q_w + ff_w : q_w + 2 * ff_w],
                rest[:, q_w + 2 * ff_w :],
            )
        )

    def gains_of(l):
        rows = gain_all[4 * l : 4 * l + 4]
        heads_gain = rows[2:].reshape(2, fsdp, part)[:, :, :small].reshape(2, fsdp * small)
        return rows[0], rows[1], jnp.pad(heads_gain, ((0, 6), (0, 0)))

    positions = positions_of(segment_ids)
    cosine, sine = rope_tables(positions, HD)
    cosine, sine = cosine[:, 0, :], sine[:, 0, :]
    seqs, length = segment_ids.shape
    tables = (
        jnp.concatenate([cosine, cosine], axis=1),
        jnp.concatenate([-sine, sine], axis=1),
        segment_ids.reshape(-1, 1),
        segment_ids.reshape(seqs, 1, length),
    )

    resid = inputs
    kept = []
    for l in range(layers):
        w_qkv, w_o, w_g, w_u, w_d = full[l]
        attn_gain, mlp_gain, head_gain = gains_of(l)
        normed, hat_a, scale_a = row_norm(resid, attn_gain)
        attn_rows = spread_rows(normed.astype(jnp.bfloat16))
        qkv = mat_dot(attn_rows, w_qkv)
        attended = attend(qkv, tables, head_gain, dims)
        resid_mid = resid + sum_rows(dot_right_t(attended, w_o))
        normed_m, hat_m, scale_m = row_norm(resid_mid, mlp_gain)
        mlp_rows = spread_rows(normed_m.astype(jnp.bfloat16))
        gate_act = mat_dot(mlp_rows, w_g)
        up_act = mat_dot(mlp_rows, w_u)
        hidden = (jax.nn.silu(gate_act) * up_act).astype(jnp.bfloat16)
        resid = resid_mid + sum_rows(dot_right_t(hidden, w_d))
        kept.append(
            (hat_a, scale_a, attn_rows, qkv, attended, hat_m, scale_m, mlp_rows, gate_act, up_act, hidden)
        )

    grad = cotangent
    grads = [None] * layers
    gain_grads = [None] * layers
    for l in reversed(range(layers)):
        w_qkv, w_o, w_g, w_u, w_d = full[l]
        attn_gain, mlp_gain, head_gain = gains_of(l)
        (hat_a, scale_a, attn_rows, qkv, attended, hat_m, scale_m, mlp_rows, gate_act, up_act, hidden) = kept[l]
        grad_half = spread_rows(grad.astype(jnp.bfloat16))
        grad_hidden = mat_dot(grad_half, w_d)
        sig = jax.nn.sigmoid(gate_act)
        grad_gate_act = (grad_hidden * up_act * sig * (1.0 + gate_act * (1.0 - sig))).astype(jnp.bfloat16)
        grad_up_act = (grad_hidden * gate_act * sig).astype(jnp.bfloat16)
        grad_normed_m = sum_rows(dot_right_t(grad_gate_act, w_g) + dot_right_t(grad_up_act, w_u))
        grad_in, grad_mlp_gain = norm_back(grad_normed_m, hat_m, scale_m, mlp_gain, (0,))
        grad_mid = grad + grad_in
        grad_mid_half = spread_rows(grad_mid.astype(jnp.bfloat16))
        grad_attended = mat_dot(grad_mid_half, w_o).astype(jnp.bfloat16)
        grad_qkv, grad_heads = attend_back(qkv, tables, head_gain, dims, grad_attended)
        grad_normed_a = sum_rows(dot_right_t(grad_qkv, w_qkv))
        grad_in, grad_attn_gain = norm_back(grad_normed_a, hat_a, scale_a, attn_gain, (0,))
        grad = grad_mid + grad_in
        rest = scatter_grads(
            jnp.concatenate(
                [
                    dot_left_t(grad_mid_half, attended).astype(jnp.bfloat16),
                    dot_left_t(mlp_rows, grad_gate_act).astype(jnp.bfloat16),
                    dot_left_t(mlp_rows, grad_up_act).astype(jnp.bfloat16),
                    dot_left_t(grad_half, hidden).astype(jnp.bfloat16),
                ],
                axis=1,
            )
        )
        lead = scatter_grads(dot_left_t(attn_rows, grad_qkv))
        grads[l] = (
            lead[:, :q_w],
            lead[:, q_w : q_w + kv_w],
            lead[:, q_w + kv_w :],
            rest[:, :q_w].T,
            rest[:, q_w : q_w + ff_w],
            rest[:, q_w + ff_w : q_w + 2 * ff_w],
            rest[:, q_w + 2 * ff_w :].T,
        )
        gain_grads[l] = jnp.concatenate(
            [grad_attn_gain, grad_mlp_gain, grad_heads[0], grad_heads[1]]
        )

    summed = lax.psum(jnp.stack(gain_grads), ("fsdp", "tp"))
    model = part * fsdp
    head = small * fsdp

    def own(lo, size, width):
        return lax.dynamic_slice_in_dim(summed[:, lo : lo + size], fsdp_idx * width, width, 1)

    stacked = [jnp.stack([grads[l][i] for l in range(layers)]) for i in range(7)]
    return (
        resid,
        grad,
        *stacked,
        own(0, model, part),
        own(model, model, part),
        own(2 * model, head, small),
        own(2 * model + head, head, small),
    )


def solution(mesh):
    return jax.shard_map(
        local,
        mesh=mesh,
        in_specs=(
            P(("fsdp", "tp"), None),
            P("fsdp", None),
            P(None, "fsdp"),
            P(None, "fsdp"),
            P(None, "fsdp"),
            P(None, "fsdp"),
            P(None, "fsdp", "tp"),
            P(None, "fsdp", "tp"),
            P(None, "fsdp", "tp"),
            P(None, "tp", "fsdp"),
            P(None, "fsdp", "tp"),
            P(None, "fsdp", "tp"),
            P(None, "tp", "fsdp"),
            P(("fsdp", "tp"), None),
        ),
        out_specs=(
            P(("fsdp", "tp"), None),
            P(("fsdp", "tp"), None),
            P(None, "fsdp", "tp"),
            P(None, "fsdp", "tp"),
            P(None, "fsdp", "tp"),
            P(None, "tp", "fsdp"),
            P(None, "fsdp", "tp"),
            P(None, "fsdp", "tp"),
            P(None, "tp", "fsdp"),
            P(None, "fsdp"),
            P(None, "fsdp"),
            P(None, "fsdp"),
            P(None, "fsdp"),
        ),
        check_vma=False,
    )
```

```python
import functools
import math

import jax
import jax.numpy as jnp
from jax import lax
from jax.experimental import pallas as pl
from jax.experimental.pallas import tpu as pltpu
from jax.sharding import PartitionSpec as P

HD = 128
DOC_MAX = 512


epsilon = 1e-06
theta_base = 1000000.0


def mat_dot(left_arg, right_arg):
    return jnp.dot(left_arg, right_arg, preferred_element_type=jnp.float32)


def dot_left_t(left_arg, right_arg):
    return lax.dot_general(
        left_arg, right_arg, (((0,), (0,)), ((), ())), preferred_element_type=jnp.float32
    )


def dot_right_t(left_arg, right_arg):
    return lax.dot_general(
        left_arg, right_arg, (((1,), (1,)), ((), ())), preferred_element_type=jnp.float32
    )


def positions_of(segment_ids):
    token_index = jnp.arange(segment_ids.shape[1], dtype=jnp.int32)[None, :]
    first_flag = jnp.concatenate(
        [
            jnp.ones((segment_ids.shape[0], 1), dtype=jnp.bool_),
            segment_ids[:, 1:] != segment_ids[:, :-1],
        ],
        axis=1,
    )
    starts = lax.cummax(jnp.where(first_flag, token_index, jnp.zeros_like(token_index)), axis=1)
    return (token_index - starts).reshape(-1)


def rope_tables(positions, head_dim):
    half_dim = head_dim // 2
    frequency = jnp.exp(
        jnp.arange(half_dim, dtype=jnp.float32) * (-2.0 * math.log(theta_base) / head_dim)
    )
    angles = positions.astype(jnp.float32)[:, None] * frequency[None, :]
    return (jnp.cos(angles)[:, None, :], jnp.sin(angles)[:, None, :])


def row_norm(operand, gain_vec):
    scale_part = lax.rsqrt(jnp.mean(operand * operand, axis=-1, keepdims=True) + epsilon)
    hat_part = operand * scale_part
    return (hat_part * gain_vec, hat_part, scale_part)


def norm_back(grad_normed, hat_part, scale_part, gain_vec, sum_axes):
    scaled = grad_normed * gain_vec
    grad_in = scale_part * (scaled - hat_part * jnp.mean(scaled * hat_part, axis=-1, keepdims=True))
    grad_gain = jnp.sum(grad_normed * hat_part, axis=sum_axes)
    return (grad_in, grad_gain)


def head_rot(operand, gain_row, cos_wide, sin_wide):
    normed, hat_part, scale_part = row_norm(operand, gain_row)
    rotated = normed * cos_wide + pltpu.roll(normed, HD // 2, 1) * sin_wide
    return rotated.astype(jnp.bfloat16), hat_part, scale_part


def head_back(grad_rot, hat_part, scale_part, gain_row, cos_wide, sin_wide):
    grad_n = grad_rot * cos_wide - pltpu.roll(grad_rot, HD // 2, 1) * sin_wide
    grad_in, grad_gain = norm_back(grad_n, hat_part, scale_part, gain_row, (0,))
    return grad_in.astype(jnp.bfloat16), grad_gain[None, :]


def block_exp(q_blk, k_win, seg_col, seg_row, row_lo, key_lo):
    rows, keys = q_blk.shape[0], k_win.shape[0]
    scores = dot_right_t(q_blk, k_win) * (HD ** (-0.5))
    u_idx = row_lo + lax.broadcasted_iota(jnp.int32, (rows, keys), 0)
    t_idx = key_lo + lax.broadcasted_iota(jnp.int32, (rows, keys), 1)
    allowed = (seg_col == seg_row) & (t_idx <= u_idx)
    powers = jnp.where(allowed, jnp.exp(scores), 0.0)
    return powers / jnp.sum(powers, axis=-1, keepdims=True)


def attend_kernel(group, rows, q_ref, k_ref, v_ref, cos_ref, sin_ref, gain_ref, sc_ref, sr_ref, o_ref):
    length = k_ref.shape[0]
    gain_q, gain_k = gain_ref[0:1, :], gain_ref[1:2, :]
    k_rot, _, _ = head_rot(k_ref[...], gain_k, cos_ref[...], sin_ref[...])
    values = v_ref[...].astype(jnp.bfloat16)
    for lo in range(0, length, rows):
        hi = lo + rows
        key_lo = max(0, lo - DOC_MAX)
        for g in range(group):
            lanes = slice(g * HD, (g + 1) * HD)
            q_rot, _, _ = head_rot(
                q_ref[lo:hi, lanes], gain_q, cos_ref[lo:hi, :], sin_ref[lo:hi, :]
            )
            probs = block_exp(
                q_rot, k_rot[key_lo:hi], sc_ref[lo:hi, :], sr_ref[0, :, key_lo:hi], lo, key_lo
            )
            o_ref[lo:hi, lanes] = mat_dot(probs.astype(jnp.bfloat16), values[key_lo:hi]).astype(
                jnp.bfloat16
            )


def attend_back_kernel(
    group, rows, heads, kv, q_ref, k_ref, v_ref, cos_ref, sin_ref, gain_ref, sc_ref, sr_ref,
    da_ref, out_ref, gg_ref, dk_ref, dv_ref,
):
    length = k_ref.shape[0]
    kv_idx = pl.program_id(1)
    gain_q, gain_k = gain_ref[0:1, :], gain_ref[1:2, :]
    k_rot, k_hat, k_scale = head_rot(k_ref[...], gain_k, cos_ref[...], sin_ref[...])
    values = v_ref[...].astype(jnp.bfloat16)
    dk_ref[...] = jnp.zeros_like(dk_ref)
    dv_ref[...] = jnp.zeros_like(dv_ref)
    gq_total = jnp.zeros((1, HD), jnp.float32)
    scale = HD ** (-0.5)
    for lo in range(0, length, rows):
        hi = lo + rows
        key_lo = max(0, lo - DOC_MAX)
        k_win, v_win = k_rot[key_lo:hi], values[key_lo:hi]
        for g in range(group):
            lanes = slice(g * HD, (g + 1) * HD)
            cos_b, sin_b = cos_ref[lo:hi, :], sin_ref[lo:hi, :]
            q_rot, q_hat, q_scale = head_rot(q_ref[lo:hi, lanes], gain_q, cos_b, sin_b)
            probs = block_exp(
                q_rot, k_win, sc_ref[lo:hi, :], sr_ref[0, :, key_lo:hi], lo, key_lo
            )
            da = da_ref[lo:hi, lanes]
            dv_ref[key_lo:hi, :] += dot_left_t(probs.astype(jnp.bfloat16), da)
            grad_probs = dot_right_t(da, v_win)
            delta = jnp.sum(probs * grad_probs, axis=-1, keepdims=True)
            ds = (probs * (grad_probs - delta) * scale).astype(jnp.bfloat16)
            dk_ref[key_lo:hi, :] += dot_left_t(ds, q_rot)
            dq, gq = head_back(mat_dot(ds, k_win), q_hat, q_scale, gain_q, cos_b, sin_b)
            gq_total = gq_total + gq
            off = pl.multiple_of((kv_idx * group + g) * HD, HD)
            out_ref[lo:hi, pl.ds(off, HD)] = dq
    dk, gk = head_back(dk_ref[...], k_hat, k_scale, gain_k, cos_ref[...], sin_ref[...])
    out_ref[:, pl.ds(pl.multiple_of((heads + kv_idx) * HD, HD), HD)] = dk
    out_ref[:, pl.ds(pl.multiple_of((heads + kv + kv_idx) * HD, HD), HD)] = dv_ref[...].astype(
        jnp.bfloat16
    )

    @pl.when((pl.program_id(0) == 0) & (kv_idx == 0))
    def _():
        gg_ref[...] = jnp.zeros_like(gg_ref)

    gg_ref[0:1, :] += gq_total
    gg_ref[1:2, :] += gk


def head_specs(length, group, heads, kv):
    return [
        pl.BlockSpec((length, group * HD), lambda s, k: (s, k)),
        pl.BlockSpec((length, HD), lambda s, k: (s, heads + k)),
        pl.BlockSpec((length, HD), lambda s, k: (s, heads + kv + k)),
        pl.BlockSpec((length, HD), lambda s, k: (s, 0)),
        pl.BlockSpec((length, HD), lambda s, k: (s, 0)),
        pl.BlockSpec((8, HD), lambda s, k: (0, 0)),
        pl.BlockSpec((length, 1), lambda s, k: (s, 0)),
        pl.BlockSpec((1, 1, length), lambda s, k: (s, 0, 0)),
    ]


def attend(qkv, tables, gains, dims):
    heads, kv = dims
    cos_wide, sin_wide, seg_col, seg_row = tables
    seqs, _, length = seg_row.shape
    group = heads // kv
    rows = min(256, length)
    tokens = seqs * length
    return pl.pallas_call(
        functools.partial(attend_kernel, group, rows),
        grid=(seqs, kv),
        in_specs=head_specs(length, group, heads, kv),
        out_specs=pl.BlockSpec((length, group * HD), lambda s, k: (s, k)),
        out_shape=jax.ShapeDtypeStruct((tokens, heads * HD), jnp.bfloat16),
        cost_estimate=pl.CostEstimate(
            flops=4 * tokens * heads * HD * 640, bytes_accessed=qkv.size * 6, transcendentals=0
        ),
        compiler_params=pltpu.CompilerParams(vmem_limit_bytes=40 * 2**20),
        name="attend",
    )(qkv, qkv, qkv, cos_wide, sin_wide, gains, seg_col, seg_row)


def attend_back(qkv, tables, gains, dims, grad_attended):
    heads, kv = dims
    cos_wide, sin_wide, seg_col, seg_row = tables
    seqs, _, length = seg_row.shape
    group = heads // kv
    rows = min(256, length)
    tokens = seqs * length
    width = (heads + 2 * kv) * HD
    return pl.pallas_call(
        functools.partial(attend_back_kernel, group, rows, heads, kv),
        grid=(seqs, kv),
        in_specs=head_specs(length, group, heads, kv)
        + [pl.BlockSpec((length, group * HD), lambda s, k: (s, k))],
        out_specs=[
            pl.BlockSpec((length, width), lambda s, k: (s, 0)),
            pl.BlockSpec((8, HD), lambda s, k: (0, 0)),
        ],
        out_shape=[
            jax.ShapeDtypeStruct((tokens, width), jnp.bfloat16),
            jax.ShapeDtypeStruct((8, HD), jnp.float32),
        ],
        scratch_shapes=[pltpu.VMEM((length, HD), jnp.float32)] * 2,
        cost_estimate=pl.CostEstimate(
            flops=10 * tokens * heads * HD * 640, bytes_accessed=qkv.size * 8, transcendentals=0
        ),
        compiler_params=pltpu.CompilerParams(vmem_limit_bytes=48 * 2**20),
        name="attend_back",
    )(qkv, qkv, qkv, cos_wide, sin_wide, gains, seg_col, seg_row, grad_attended)


def meet_peers(me, n):
    barrier = pltpu.get_barrier_semaphore()
    for d in range(1, n):
        pl.semaphore_signal(
            barrier,
            inc=1,
            device_id={"tp": lax.rem(me + d, n)},
            device_id_type=pl.DeviceIdType.MESH,
        )
    pl.semaphore_wait(barrier, n - 1)


def spread_kernel(n, x_ref, o_ref, send_sem, recv_sem):
    me = lax.axis_index("tp")
    rows = x_ref.shape[0]
    meet_peers(me, n)
    own = pl.ds(pl.multiple_of(me * rows, rows), rows)
    copies = []
    for d in range(1, n):
        copy = pltpu.make_async_remote_copy(
            src_ref=x_ref,
            dst_ref=o_ref.at[own, :],
            send_sem=send_sem.at[d - 1],
            recv_sem=recv_sem.at[d - 1],
            device_id={"tp": lax.rem(me + d, n)},
            device_id_type=pl.DeviceIdType.MESH,
        )
        copy.start()
        copies.append(copy)
    o_ref[own, :] = x_ref[...]
    for copy in copies:
        copy.wait()


def sum_kernel(n, x_ref, o_ref, slots, send_sem, recv_sem):
    me = lax.axis_index("tp")
    rows = o_ref.shape[0]
    meet_peers(me, n)
    copies = []
    for d in range(1, n):
        peer = lax.rem(me + d, n)
        copy = pltpu.make_async_remote_copy(
            src_ref=x_ref.at[pl.ds(pl.multiple_of(peer * rows, rows), rows), :],
            dst_ref=slots.at[d - 1],
            send_sem=send_sem.at[d - 1],
            recv_sem=recv_sem.at[d - 1],
            device_id={"tp": peer},
            device_id_type=pl.DeviceIdType.MESH,
        )
        copy.start()
        copies.append(copy)
    for copy in copies:
        copy.wait()
    total = x_ref[pl.ds(pl.multiple_of(me * rows, rows), rows), :].astype(jnp.float32)
    for d in range(1, n):
        total = total + slots[d - 1].astype(jnp.float32)
    o_ref[...] = total


def link_params(collective_id):
    return pltpu.CompilerParams(
        collective_id=collective_id, has_side_effects=True, vmem_limit_bytes=24 * 2**20
    )


def link_cost(size):
    return pl.CostEstimate(flops=0, bytes_accessed=40 * size, transcendentals=0)


VMEM_SPEC = pl.BlockSpec(memory_space=pltpu.VMEM)


def spread_rows(local_rows):
    n = lax.axis_size("tp")
    rows, width = local_rows.shape
    return pl.pallas_call(
        functools.partial(spread_kernel, n),
        in_specs=[VMEM_SPEC],
        out_specs=VMEM_SPEC,
        out_shape=jax.ShapeDtypeStruct((n * rows, width), local_rows.dtype),
        scratch_shapes=[pltpu.SemaphoreType.DMA((n - 1,)), pltpu.SemaphoreType.DMA((n - 1,))],
        compiler_params=link_params(0),
        cost_estimate=link_cost(n * rows * width),
        name="spread_rows",
    )(local_rows)


def sum_rows(partial_rows):
    n = lax.axis_size("tp")
    rows, width = partial_rows.shape[0] // n, partial_rows.shape[1]
    return pl.pallas_call(
        functools.partial(sum_kernel, n),
        in_specs=[VMEM_SPEC],
        out_specs=VMEM_SPEC,
        out_shape=jax.ShapeDtypeStruct((rows, width), jnp.float32),
        scratch_shapes=[
            pltpu.VMEM((n - 1, rows, width), jnp.bfloat16),
            pltpu.SemaphoreType.DMA((n - 1,)),
            pltpu.SemaphoreType.DMA((n - 1,)),
        ],
        compiler_params=link_params(1),
        cost_estimate=link_cost(n * rows * width),
        name="sum_rows",
    )(partial_rows.astype(jnp.bfloat16))


def gather_weights(block):
    return lax.all_gather(block, "fsdp", axis=0, tiled=True)


def scatter_grads(block):
    return lax.psum_scatter(
        block.astype(jnp.bfloat16), "fsdp", scatter_dimension=0, tiled=True
    ).astype(jnp.float32)


def local(
    inputs, segment_ids, attn_norm, mlp_norm, query_norm, key_norm, w_query, w_key, w_value,
    w_out, w_gate, w_up, w_down, cotangent,
):
    layers = w_query.shape[0]
    fsdp = lax.axis_size("fsdp")
    fsdp_idx = lax.axis_index("fsdp")
    part = attn_norm.shape[1]
    small = query_norm.shape[1]
    q_w, kv_w = w_query.shape[2], w_key.shape[2]
    ff_w = w_gate.shape[2]
    dims = (q_w // HD, kv_w // HD)
    qkv_w = q_w + 2 * kv_w

    columns = []
    for l in range(layers):
        columns += [
            attn_norm[l],
            mlp_norm[l],
            jnp.pad(query_norm[l], (0, part - small)),
            jnp.pad(key_norm[l], (0, part - small)),
        ]
    gain_block = jnp.stack(columns, axis=1)
    gain_block = jnp.pad(gain_block, ((0, 0), (0, -gain_block.shape[1] % HD)))
    gain_w = gain_block.shape[1]

    def qkv_block(l):
        return [w_query[l], w_key[l], w_value[l]]

    def rest_block(l):
        return [w_out[l].T, w_gate[l], w_up[l], w_down[l].T]

    full = []
    for l in range(layers):
        lead = gather_weights(
            jnp.concatenate(qkv_block(l) + ([gain_block] if l == 0 else []), axis=1)
        )
        if l == 0:
            gain_all = lead[:, qkv_w:].T.astype(jnp.float32)
        rest = gather_weights(jnp.concatenate(rest_block(l), axis=1))
        full.append(
            (
                lead[:, :qkv_w],
                rest[:, :q_w],
                rest[:, q_w : q_w + ff_w],
                rest[:, q_w + ff_w : q_w + 2 * ff_w],
                rest[:, q_w + 2 * ff_w :],
            )
        )

    def gains_of(l):
        rows = gain_all[4 * l : 4 * l + 4]
        heads_gain = rows[2:].reshape(2, fsdp, part)[:, :, :small].reshape(2, fsdp * small)
        return rows[0], rows[1], jnp.pad(heads_gain, ((0, 6), (0, 0)))

    positions = positions_of(segment_ids)
    cosine, sine = rope_tables(positions, HD)
    cosine, sine = cosine[:, 0, :], sine[:, 0, :]
    seqs, length = segment_ids.shape
    tables = (
        jnp.concatenate([cosine, cosine], axis=1),
        jnp.concatenate([-sine, sine], axis=1),
        segment_ids.reshape(-1, 1),
        segment_ids.reshape(seqs, 1, length),
    )

    resid = inputs
    kept = []
    for l in range(layers):
        w_qkv, w_o, w_g, w_u, w_d = full[l]
        attn_gain, mlp_gain, head_gain = gains_of(l)
        normed, hat_a, scale_a = row_norm(resid, attn_gain)
        attn_rows = spread_rows(normed.astype(jnp.bfloat16))
        qkv = mat_dot(attn_rows, w_qkv)
        attended = attend(qkv, tables, head_gain, dims)
        resid_mid = resid + sum_rows(dot_right_t(attended, w_o))
        normed_m, hat_m, scale_m = row_norm(resid_mid, mlp_gain)
        mlp_rows = spread_rows(normed_m.astype(jnp.bfloat16))
        gate_act = mat_dot(mlp_rows, w_g)
        up_act = mat_dot(mlp_rows, w_u)
        hidden = (jax.nn.silu(gate_act) * up_act).astype(jnp.bfloat16)
        resid = resid_mid + sum_rows(dot_right_t(hidden, w_d))
        kept.append(
            (hat_a, scale_a, attn_rows, qkv, attended, hat_m, scale_m, mlp_rows, gate_act, up_act, hidden)
        )

    def split_grads(lead, rest):
        return (
            lead[:, :q_w],
            lead[:, q_w : q_w + kv_w],
            lead[:, q_w + kv_w :],
            rest[:, :q_w].T,
            rest[:, q_w : q_w + ff_w],
            rest[:, q_w + ff_w : q_w + 2 * ff_w],
            rest[:, q_w + 2 * ff_w :].T,
        )

    grad = cotangent
    pending = None
    grads = [None] * layers
    gain_grads = [None] * layers
    for l in reversed(range(layers)):
        w_qkv, w_o, w_g, w_u, w_d = full[l]
        attn_gain, mlp_gain, head_gain = gains_of(l)
        (hat_a, scale_a, attn_rows, qkv, attended, hat_m, scale_m, mlp_rows, gate_act, up_act, hidden) = kept[l]
        grad_half = spread_rows(grad.astype(jnp.bfloat16))
        grad_hidden = mat_dot(grad_half, w_d)
        sig = jax.nn.sigmoid(gate_act)
        grad_gate_act = (grad_hidden * up_act * sig * (1.0 + gate_act * (1.0 - sig))).astype(jnp.bfloat16)
        grad_up_act = (grad_hidden * gate_act * sig).astype(jnp.bfloat16)
        grad_normed_m = sum_rows(dot_right_t(grad_gate_act, w_g) + dot_right_t(grad_up_act, w_u))
        if pending is not None:
            grad_normed_m, rest_done = lax.optimization_barrier((grad_normed_m, pending[1]))
        grad_in, grad_mlp_gain = norm_back(grad_normed_m, hat_m, scale_m, mlp_gain, (0,))
        grad_mid = grad + grad_in
        grad_mid_half = spread_rows(grad_mid.astype(jnp.bfloat16))
        if pending is not None:
            grad_mid_half, lead_done = lax.optimization_barrier((grad_mid_half, pending[0]))
            grads[l + 1] = split_grads(lead_done, rest_done)
        grad_attended = mat_dot(grad_mid_half, w_o).astype(jnp.bfloat16)
        rest_block = jnp.concatenate(
                [
                    dot_left_t(grad_mid_half, attended).astype(jnp.bfloat16),
                    dot_left_t(mlp_rows, grad_gate_act).astype(jnp.bfloat16),
                    dot_left_t(mlp_rows, grad_up_act).astype(jnp.bfloat16),
                    dot_left_t(grad_half, hidden).astype(jnp.bfloat16),
                ],
                axis=1,
            )
        grad_attended, rest_block = lax.optimization_barrier((grad_attended, rest_block))
        rest = scatter_grads(rest_block)
        grad_qkv, grad_heads = attend_back(qkv, tables, head_gain, dims, grad_attended)
        back_a, lead_block = lax.optimization_barrier(
            (
                dot_right_t(grad_qkv, w_qkv).astype(jnp.bfloat16),
                dot_left_t(attn_rows, grad_qkv).astype(jnp.bfloat16),
            )
        )
        lead = scatter_grads(lead_block)
        grad_normed_a = sum_rows(back_a)
        grad_in, grad_attn_gain = norm_back(grad_normed_a, hat_a, scale_a, attn_gain, (0,))
        grad = grad_mid + grad_in
        pending = (lead, rest)
        gain_grads[l] = jnp.concatenate(
            [grad_attn_gain, grad_mlp_gain, grad_heads[0], grad_heads[1]]
        )

    grads[0] = split_grads(*pending)
    summed = lax.psum(jnp.stack(gain_grads), ("fsdp", "tp"))
    model = part * fsdp
    head = small * fsdp

    def own(lo, size, width):
        return lax.dynamic_slice_in_dim(summed[:, lo : lo + size], fsdp_idx * width, width, 1)

    stacked = [jnp.stack([grads[l][i] for l in range(layers)]) for i in range(7)]
    return (
        resid,
        grad,
        *stacked,
        own(0, model, part),
        own(model, model, part),
        own(2 * model, head, small),
        own(2 * model + head, head, small),
    )


def solution(mesh):
    return jax.shard_map(
        local,
        mesh=mesh,
        in_specs=(
            P(("fsdp", "tp"), None),
            P("fsdp", None),
            P(None, "fsdp"),
            P(None, "fsdp"),
            P(None, "fsdp"),
            P(None, "fsdp"),
            P(None, "fsdp", "tp"),
            P(None, "fsdp", "tp"),
            P(None, "fsdp", "tp"),
            P(None, "tp", "fsdp"),
            P(None, "fsdp", "tp"),
            P(None, "fsdp", "tp"),
            P(None, "tp", "fsdp"),
            P(("fsdp", "tp"), None),
        ),
        out_specs=(
            P(("fsdp", "tp"), None),
            P(("fsdp", "tp"), None),
            P(None, "fsdp", "tp"),
            P(None, "fsdp", "tp"),
            P(None, "fsdp", "tp"),
            P(None, "tp", "fsdp"),
            P(None, "fsdp", "tp"),
            P(None, "fsdp", "tp"),
            P(None, "tp", "fsdp"),
            P(None, "fsdp"),
            P(None, "fsdp"),
            P(None, "fsdp"),
            P(None, "fsdp"),
        ),
        check_vma=False,
    )
```
